1024 devices in a mesh: tile: 128 (over z, x, core), lev: 8 (over y).
Axes of the slice: x: 8, y: 8, z: 8, core: 2. Of those that a mesh axis runs over, the one named last changes fastest.
Arguments:
- theta: float32 [128, 32, 16384], P('lev', None, 'tile'), may hold values from -6 to 6
- thickness: float32 [128, 32, 16384], P('lev', None, 'tile'), may hold values from 0.5 to 1.5
- wind: float32 [128, 32, 16384], P('lev', None, 'tile'), may hold values from -6 to 6
- surface: float32 [32, 16384], P(None, 'tile'), may hold values from -6 to 6
- trigger: int32 [32, 16384], P(None, 'tile'), may hold values 0 or 1
- closure: int32 [32, 16384], P(None, 'tile'), may hold values from 0 to 2
- closure_weights: bfloat16 [4, 128, 128], replicated, may hold values from -0.5 to 0.5
Outputs:
- pressure: float32 [128, 32, 16384], P('lev', None, 'tile')
- wind_next: float32 [128, 32, 16384], P('lev', None, 'tile')
- heating: bfloat16 [128, 32, 16384], P('lev', None, 'tile')
The draws below stay inside these ranges and needn't reach their ends.
Inputs may be any that keep to these rules, and one draw needn't show every extreme that they name: trigger[r, c] is 0 or 1 in every draw. closure[r, c] is one of 0 .. 2 in every draw.
All inputs are finite; a program needn't handle non-finite values. No bound on the sum of `trigger` on one device may be relied on, other than what follows from the above.
Results may differ from the reference program's by a relative error of at most 0.0049.
Values may be sent and summed in bfloat16 or wider, within the bound.
No kernel may reach another device: no remote copies, remote signals or barrier semaphores. Data moves between devices by JAX's collectives and lax.ppermute only.
A program may use at most 32 MiB of HBM per device.

```python
import jax
import jax.numpy as jnp
from jax import lax

LEVELS = 128
CLOSURES = 3
SUBSTEPS = 6
ROWS = 32
LONS = 16384


def with_ends(array, rng, smallest, top_value):
    index_at = [jax.random.randint(jax.random.fold_in(rng, axis), (), 0, length) for axis, length in enumerate(array.shape)]
    widest = array.shape.index(max(array.shape))
    neighbour = index_at[:widest] + [(index_at[widest] + 1) % array.shape[widest]] + index_at[widest + 1:]
    return array.at[tuple(index_at)].set(smallest).at[tuple(neighbour)].set(top_value)


def block_levels(key, dims, split, least, largest):
    gain, own = 1.0, jax.random.fold_in(key, 6)
    for position, shards_of in split:
        draws = jnp.exp(jax.random.uniform(jax.random.fold_in(own, position), (shards_of,), jnp.float32, least / len(split), largest / len(split)))
        gain = gain * jnp.repeat(draws, dims[position] // shards_of).reshape([-1 if axis == position else 1 for axis in range(len(dims))])
    return gain


def centred(rng, shape, spread, bound, split=(), dtype=jnp.bfloat16):
    entries = spread * jax.random.normal(rng, shape, jnp.float32)
    if split:
        entries = entries * block_levels(rng, shape, split, -0.22, 0.18)
    return jnp.clip(entries, -bound, bound).astype(dtype)


def setup_inputs(seed: int = 0) -> dict:
    streams_of = jax.random.split(jax.random.key(seed), 8)
    theta = centred(streams_of[0], (LEVELS, ROWS, LONS), 1.0, 6.0, ((0, 8), (2, 128)), jnp.float32)
    thickness = jnp.clip(0.5 + 1.0 * jax.random.uniform(streams_of[1], (LEVELS, ROWS, LONS), jnp.float32) ** block_levels(streams_of[1], (LEVELS, ROWS, LONS), ((0, 8), (2, 128)), -0.2, 0.2), 0.5, 1.5)
    wind = centred(streams_of[2], (LEVELS, ROWS, LONS), 1.0, 6.0, ((0, 8), (2, 128)), jnp.float32)
    surface = centred(streams_of[3], (ROWS, LONS), 1.0, 6.0, ((1, 128),), jnp.float32)
    trigger = with_ends((jax.random.randint(streams_of[4], (ROWS, LONS), 0, 2) < 1).astype(jnp.int32), jax.random.fold_in(streams_of[4], 1), 0, 1)
    closure = with_ends(jax.random.randint(streams_of[5], (ROWS, LONS), 0, CLOSURES), jax.random.fold_in(streams_of[5], 1), 0, CLOSURES - 1).astype(jnp.int32)
    closure_weights = centred(streams_of[6], (CLOSURES + 1, LEVELS, LEVELS), LEVELS ** -0.5, 0.5)
    return dict(theta=theta, thickness=thickness, wind=wind, surface=surface, trigger=trigger, closure=closure, closure_weights=closure_weights)


courant = 0.9


def reference(theta, thickness, wind, surface, trigger, closure, closure_weights):
    thermal = theta * thickness * (LEVELS ** -0.5)
    suffix = lax.cumsum(thermal, axis=0, reverse=True) - thermal
    geopot = surface[None, :, :] + suffix + 0.5 * thermal
    pressure = geopot
    velocity = wind
    for substep in range(SUBSTEPS):
        velocity = velocity - courant * (jnp.roll(pressure, -1, axis=2) - pressure)
        pressure = pressure - courant * (velocity - jnp.roll(velocity, 1, axis=2))
    column = theta.astype(jnp.bfloat16).reshape((LEVELS, ROWS * LONS))
    boundary = jnp.dot(closure_weights[CLOSURES], column, preferred_element_type=jnp.float32).reshape((LEVELS, ROWS, LONS))
    convect = jnp.zeros(theta.shape, jnp.float32)
    for scheme in range(CLOSURES):
        answer = jnp.dot(closure_weights[scheme], column, preferred_element_type=jnp.float32).reshape((LEVELS, ROWS, LONS))
        convect = convect + jnp.where(closure[None, :, :] == scheme, answer, jnp.float32(0.0))
    heating = (boundary + trigger.astype(jnp.float32)[None, :, :] * convect).astype(jnp.bfloat16)
    return pressure, velocity, heating
```

```python
import jax
import jax.numpy as jnp
from jax import lax
from jax.experimental import pallas as pl
from jax.experimental.pallas import tpu as pltpu
from jax.sharding import PartitionSpec as P

LEVELS = 128
SUBSTEPS = 6
COURANT = 0.9
SCALE = LEVELS ** (-0.5)
PEERS = 8
OWN = 16
ROWS = 32
LANES = 128
BAND = 4
FIRST = 80
SECOND = 96
BF16 = jnp.bfloat16
F32 = jnp.float32


def lanes_of(shape):
    return lax.broadcasted_iota(jnp.int32, shape, len(shape) - 1)


def rows_of(shape):
    return lax.broadcasted_iota(jnp.int32, shape, len(shape) - 2)


def turned(x, shift):
    return pltpu.roll(x, shift % LANES, 1)


def halves_swapped(x):
    return pltpu.roll(x, 4, 0)


def three_parts(x):
    high = x.astype(BF16).astype(F32)
    rest = x - high
    middle = rest.astype(BF16).astype(F32)
    return high, middle, rest - middle


def sub(a, b):
    return a - COURANT * b


def substeps(pressure, wind):
    for _ in range(SUBSTEPS):
        wind = sub(wind, turned(pressure, -1) - pressure)
        pressure = sub(pressure, wind - turned(wind, 1))
    return pressure, wind


def windowed(main, left, right):
    lane = lanes_of(main.shape)
    return jnp.where(
        lane < 6,
        left,
        jnp.where(lane < 32, turned(main, 6), jnp.where(lane < 76, turned(main, 76), right)),
    )


def edges_in(main, window):
    lane = lanes_of(main.shape)
    return jnp.where(
        lane < 6, turned(window, -6), jnp.where(lane >= 122, turned(window, 52), main)
    )


def send_columns(theta, thickness, out):
    total = jnp.zeros((ROWS, LANES), F32)
    for level in range(OWN):
        at = pl.ds(level * ROWS, ROWS)
        total = total + theta[at, :] * thickness[at, :] * SCALE
    for row in range(ROWS):
        picked = theta[pl.ds(row, OWN, stride=ROWS), :]
        out[row // BAND, pl.ds(OWN * (row % BAND), OWN), :] = picked.astype(BF16)
    top = rows_of((8, LANES)) < 4
    for group in range(4):
        high, middle, low = three_parts(total[8 * group : 8 * group + 8])
        first = jnp.where(top, high, halves_swapped(middle))
        second = jnp.where(top, halves_swapped(high), middle)
        out[2 * group, 64:80, :] = jnp.concatenate([first, jnp.where(top, low, 0.0)]).astype(BF16)
        out[2 * group + 1, 64:80, :] = jnp.concatenate(
            [second, jnp.where(top, halves_swapped(low), 0.0)]
        ).astype(BF16)


def send_borders(theta, thickness, wind, surface, to_right, to_left):
    lane = lanes_of((ROWS, LANES))
    zero = jnp.zeros((ROWS, LANES), F32)
    below = zero
    packed = [[zero, zero], [zero, zero]]
    for level in reversed(range(OWN)):
        at = pl.ds(level * ROWS, ROWS)
        thermal = theta[at, :] * thickness[at, :] * SCALE
        fields = (below + 0.5 * thermal, wind[at, :])
        below = below + thermal
        here = (lane >= 8 * level) & (lane < 8 * level + 8)
        for index, field in enumerate(fields):
            packed[0][index] = jnp.where(here, turned(field, 8 * level - 122), packed[0][index])
            packed[1][index] = jnp.where(here, turned(field, 8 * level), packed[1][index])
    ground = surface[...]
    for out, side, lead, first in ((to_right, 0, 0, 122), (to_left, 1, 8, 0)):
        out[0:32, :] = packed[side][0]
        out[32:64, :] = packed[side][1]
        sums = jnp.where((lane >= lead) & (lane < lead + 6), turned(below, lead - first), 0.0)
        out[64:96, :] = jnp.where(
            (lane >= lead + 16) & (lane < lead + 22), turned(ground, lead + 16 - first), sums
        )


def send_heating(got, trigger, closure, weights, from_left, from_right, out, stacked):
    lane = lanes_of((ROWS, LANES))
    me = lax.axis_index("lev")
    flags = trigger[pl.ds(BAND * me, BAND), :].astype(F32)
    scheme = closure[pl.ds(BAND * me, BAND), :]
    for row in range(BAND):
        chosen = [
            jnp.broadcast_to(
                jnp.where(scheme[row : row + 1] == s, flags[row : row + 1], 0.0), (OWN, LANES)
            ).astype(BF16)
            for s in range(3)
        ]
        columns = pl.ds(LANES * row, LANES)
        for peer in range(PEERS):
            block = got[peer, pl.ds(OWN * row, OWN), :]
            for s in range(3):
                stacked[pl.ds(LEVELS * s + OWN * peer, OWN), columns] = block * chosen[s]
            stacked[pl.ds(LEVELS * 3 + OWN * peer, OWN), columns] = block
    wide = jnp.concatenate([weights[s] for s in range(4)], axis=1)
    answer = jnp.dot(wide, stacked[...], preferred_element_type=F32).astype(BF16)
    for peer in range(PEERS):
        for row in range(BAND):
            out[peer, pl.ds(OWN * row, OWN), :] = answer[
                OWN * peer : OWN * peer + OWN, LANES * row : LANES * row + LANES
            ]
    borders = from_left[64:96, :] + from_right[64:96, :]
    borders = jnp.where(lane < 16, borders, 0.0)
    folded = borders[0:8]
    for group in range(1, 4):
        folded = folded + turned(borders[8 * group : 8 * group + 8], 32 * group)
    top = rows_of((8, LANES)) < 4
    bottom = halves_swapped(folded) + turned(folded, 16)
    higher = jnp.zeros((8, LANES), F32)
    for peer in reversed(range(PEERS)):
        high, middle, low = three_parts(jnp.where(top, higher, bottom))
        out[peer, 64:80, :] = jnp.concatenate([high, middle]).astype(BF16)
        out[peer, 80:96, :] = jnp.concatenate([low, jnp.zeros_like(low)]).astype(BF16)
        parts = got[peer, 64:80, :].astype(F32)
        higher = higher + ((parts[0:8] + halves_swapped(parts[0:8])) + parts[8:16])


def local_substeps(
    theta, thickness, wind, surface, from_left, from_right, out_p, out_w, main_p, main_w, side_p, side_w
):
    ground = surface[...]
    left_ground = turned(from_left[64:96, :], -16)
    right_ground = turned(from_right[64:96, :], 76 - 24)
    below = jnp.zeros((ROWS, LANES), F32)
    for level in reversed(range(OWN)):
        at = pl.ds(level * ROWS, ROWS)
        thermal = theta[at, :] * thickness[at, :] * SCALE
        p = ground + (below + 0.5 * thermal)
        below = below + thermal
        main_p[at, :] = p
        side_p[at, :] = windowed(
            p,
            turned(from_left[0:32, :], -8 * level) + left_ground,
            turned(from_right[0:32, :], 76 - 8 * level) + right_ground,
        )
        side_w[at, :] = windowed(
            wind[at, :],
            turned(from_left[32:64, :], -8 * level),
            turned(from_right[32:64, :], 76 - 8 * level),
        )
    p, w = substeps(main_p[...], wind[...])
    main_p[...] = p
    main_w[...] = w
    p, w = substeps(side_p[...], side_w[...])
    out_p[...] = edges_in(main_p[...], p)
    out_w[...] = edges_in(main_w[...], w)


def finish(got, local_p, local_w, out_p, out_w, out_h, rows_first):
    me = lax.axis_index("lev")
    top = rows_of((8, LANES)) < 4
    beyond = jnp.zeros((8, LANES), F32)
    pieces = []
    for peer in range(PEERS):
        tail = got[peer, 64:96, :].astype(F32)
        piece = (tail[0:8] + tail[8:16]) + tail[16:24]
        pieces.append(piece)
        beyond = beyond + jnp.where(me < peer, 1.0, 0.0) * piece
    unfolded = jnp.where(top, halves_swapped(beyond), turned(beyond, -16))
    main = jnp.concatenate(
        [
            jnp.where(top, pieces[2 * group], halves_swapped(pieces[2 * group + 1]))
            for group in range(4)
        ]
    )
    border = jnp.concatenate([turned(unfolded, -32 * group) for group in range(4)])
    side = windowed(main, border, turned(border, 76 - 8))
    zero = jnp.zeros((ROWS, LANES), F32)
    add_p, add_w = substeps(main, zero)
    side_p, side_w = substeps(side, zero)
    add_p = edges_in(add_p, side_p)
    add_w = edges_in(add_w, side_w)
    for level in range(OWN):
        at = pl.ds(level * ROWS, ROWS)
        out_p[at, :] = local_p[at, :] + add_p
        out_w[at, :] = local_w[at, :] + add_w
    for peer in range(PEERS):
        rows_first[pl.ds(64 * peer, 64), :] = got[peer, 0:64, :].astype(F32)
    for level in range(OWN):
        out_h[pl.ds(level * ROWS, ROWS), :] = rows_first[pl.ds(level, ROWS, stride=OWN), :].astype(
            BF16
        )


def call(kernel, outs, scratch=(), flops=100000, moved=1000000, room=8 << 20):
    return pl.pallas_call(
        kernel,
        out_shape=tuple(jax.ShapeDtypeStruct(s, d) for s, d in outs),
        scratch_shapes=[pltpu.VMEM(s, d) for s, d in scratch],
        compiler_params=pltpu.CompilerParams(vmem_limit_bytes=room),
        cost_estimate=pl.CostEstimate(flops=flops, bytes_accessed=moved, transcendentals=0),
    )


def shards(theta, thickness, wind, surface, trigger, closure, closure_weights):
    flat = (OWN * ROWS, LANES)
    theta, thickness, wind = (x.reshape(flat) for x in (theta, thickness, wind))
    tiles = lax.axis_size("tile")
    (columns,) = call(send_columns, [((PEERS, FIRST, LANES), BF16)], room=60 << 20)(theta, thickness)
    columns = lax.all_to_all(columns, "lev", 0, 0, tiled=True)
    to_right, to_left = call(send_borders, [((96, LANES), F32)] * 2)(
        theta, thickness, wind, surface
    )
    from_left = lax.ppermute(to_right, "tile", [(i, (i + 1) % tiles) for i in range(tiles)])
    from_right = lax.ppermute(to_left, "tile", [((i + 1) % tiles, i) for i in range(tiles)])
    (heats,) = call(
        send_heating, [((PEERS, SECOND, LANES), BF16)], [((512, 512), BF16)], flops=70000000
    )(columns, trigger, closure, closure_weights, from_left, from_right)
    heats = lax.all_to_all(heats, "lev", 0, 0, tiled=True)
    local_p, local_w = call(local_substeps, [(flat, F32)] * 2, [(flat, F32)] * 4, flops=20000000)(
        theta, thickness, wind, surface, from_left, from_right
    )
    pressure, wind_next, heating = call(
        finish, [(flat, F32), (flat, F32), (flat, BF16)], [(flat, F32)]
    )(heats, local_p, local_w)
    shape = (OWN, ROWS, LANES)
    return pressure.reshape(shape), wind_next.reshape(shape), heating.reshape(shape)


def solution(mesh):
    in_specs = (
        P("lev", None, "tile"),
        P("lev", None, "tile"),
        P("lev", None, "tile"),
        P(None, "tile"),
        P(None, "tile"),
        P(None, "tile"),
        P(),
    )
    out_specs = (P("lev", None, "tile"), P("lev", None, "tile"), P("lev", None, "tile"))
    return jax.shard_map(shards, mesh=mesh, in_specs=in_specs, out_specs=out_specs, check_vma=False)
```

```python
import jax
import jax.numpy as jnp
from jax import lax
from jax.experimental import pallas as pl
from jax.experimental.pallas import tpu as pltpu
from jax.sharding import PartitionSpec as P


LEVELS = 128
SUBSTEPS = 6
COURANT = 0.9
SCALE = LEVELS ** (-0.5)
PEERS = 8
OWN = 16
ROWS = 32
LANES = 128
BAND = 4
PIECE = 88
BF16 = jnp.bfloat16
F32 = jnp.float32


def lanes_of(shape):
    return lax.broadcasted_iota(jnp.int32, shape, len(shape) - 1)


def rows_of(shape):
    return lax.broadcasted_iota(jnp.int32, shape, len(shape) - 2)


def turned(x, shift):
    return pltpu.roll(x, shift % LANES, 1)


def three_parts(x):
    high = x.astype(BF16).astype(F32)
    rest = x - high
    middle = rest.astype(BF16).astype(F32)
    return high, middle, rest - middle


def sub(a, b):
    return a - COURANT * b


def substeps(pressure, wind):
    for _ in range(SUBSTEPS):
        wind = sub(wind, turned(pressure, -1) - pressure)
        pressure = sub(pressure, wind - turned(wind, 1))
    return pressure, wind


def windowed(main, left, right):
    lane = lanes_of(main.shape)
    return jnp.where(
        lane < 6,
        left,
        jnp.where(lane < 32, turned(main, 6), jnp.where(lane < 76, turned(main, 76), right)),
    )


def edges_in(main, window):
    lane = lanes_of(main.shape)
    return jnp.where(
        lane < 6, turned(window, -6), jnp.where(lane >= 122, turned(window, 52), main)
    )


def odd_tile():
    return lax.rem(lax.axis_index("tile"), 2) == 1


def by_side(right, if_right, if_left):
    return jnp.where(right, if_right % LANES, if_left % LANES)


def swung(x, right, if_right, if_left):
    return pltpu.roll(x, by_side(right, if_right, if_left), 1)


def folded(border):
    kept = jnp.where(lanes_of(border.shape) < 6, border, 0.0)
    out = kept[0:8]
    for group in range(1, 4):
        out = out + turned(kept[8 * group : 8 * group + 8], 8 * group)
    return out


def unfolded(fold):
    return jnp.concatenate([turned(fold, -8 * group) for group in range(4)])


def halves_swapped(x):
    return pltpu.roll(x, 4, 0)


def in_low_half(fold):
    return halves_swapped(fold) + turned(fold, 32)


def from_low_half(fold):
    top = rows_of(fold.shape) < 4
    return jnp.where(top, halves_swapped(fold), turned(fold, -32))


def top_half():
    return rows_of((8, LANES)) < 4


def send_parts(out, peer, x):
    high, middle, low = three_parts(x)
    out[peer, 64:80, :] = jnp.concatenate([high, middle]).astype(BF16)
    out[peer, 80:88, :] = low.astype(BF16)


def got_parts(got, peer):
    pair = got[peer, 64:80, :].astype(F32)
    return (pair[0:8] + pair[8:16]) + got[peer, 80:88, :].astype(F32)


def send_columns(theta, thickness, out):
    total = jnp.zeros((ROWS, LANES), F32)
    for level in range(OWN):
        at = pl.ds(level * ROWS, ROWS)
        total = total + theta[at, :] * thickness[at, :] * SCALE
    for row in range(ROWS):
        picked = theta[pl.ds(row, OWN, stride=ROWS), :]
        out[row // BAND, pl.ds(OWN * (row % BAND), OWN), :] = picked.astype(BF16)
    border = in_low_half(folded(swung(total, odd_tile(), -122, 0)))
    for group in range(4):
        rows = total[8 * group : 8 * group + 8]
        send_parts(out, 2 * group, jnp.where(top_half(), rows, border))
        send_parts(out, 2 * group + 1, jnp.where(top_half(), halves_swapped(rows), border))


def send_borders(theta, thickness, wind, surface, to_chip, to_core):
    lane = lanes_of((ROWS, LANES))
    zero = jnp.zeros((ROWS, LANES), F32)
    ground = surface[...]
    below = zero
    packed = [[zero, zero], [zero, zero]]
    for level in reversed(range(OWN)):
        at = pl.ds(level * ROWS, ROWS)
        thermal = theta[at, :] * thickness[at, :] * SCALE
        fields = (ground + (below + 0.5 * thermal), wind[at, :])
        below = below + thermal
        here = (lane >= 8 * level) & (lane < 8 * level + 8)
        for index, field in enumerate(fields):
            packed[0][index] = jnp.where(here, turned(field, 8 * level - 122), packed[0][index])
            packed[1][index] = jnp.where(here, turned(field, 8 * level), packed[1][index])
    odd = odd_tile()
    for index in range(2):
        at = pl.ds(ROWS * index, ROWS)
        to_chip[at, :] = jnp.where(odd, packed[0][index], packed[1][index])
        to_core[at, :] = jnp.where(odd, packed[1][index], packed[0][index])
    to_core[64:72, :] = folded(swung(below, odd, 0, -122))


def send_heating(got, trigger, closure, weights, from_core, raw, out, to_chip, stacked):
    me = lax.axis_index("lev")
    flags = trigger[pl.ds(BAND * me, BAND), :].astype(F32)
    scheme = closure[pl.ds(BAND * me, BAND), :]
    for row in range(BAND):
        chosen = [
            jnp.broadcast_to(
                jnp.where(scheme[row : row + 1] == s, flags[row : row + 1], 0.0), (OWN, LANES)
            ).astype(BF16)
            for s in range(3)
        ]
        columns = pl.ds(LANES * row, LANES)
        for peer in range(PEERS):
            block = got[peer, pl.ds(OWN * row, OWN), :]
            for s in range(3):
                stacked[pl.ds(LEVELS * s + OWN * peer, OWN), columns] = block * chosen[s]
            stacked[pl.ds(LEVELS * 3 + OWN * peer, OWN), columns] = block
    wide = jnp.concatenate([weights[s] for s in range(4)], axis=1)
    answer = jnp.dot(wide, stacked[...], preferred_element_type=F32).astype(BF16)
    for peer in range(PEERS):
        for row in range(BAND):
            out[peer, pl.ds(OWN * row, OWN), :] = answer[
                OWN * peer : OWN * peer + OWN, LANES * row : LANES * row + LANES
            ]
    core_border = in_low_half(from_core[64:72, :])
    higher = jnp.zeros((8, LANES), F32)
    beyond = jnp.zeros((8, LANES), F32)
    for peer in reversed(range(PEERS)):
        send_parts(out, peer, jnp.where(top_half(), higher, core_border))
        part = got_parts(got, peer)
        higher = higher + part
        beyond = beyond + jnp.where(me < peer, 1.0, 0.0) * part
    to_chip[0:64, :] = raw[...]
    to_chip[64:72, :] = from_low_half(beyond)


def slot(level):
    return 32 * (level % 4)


def local_substeps(
    theta, thickness, wind, surface, from_core, out_p, out_w, chip_p, chip_w, core_p, core_w
):
    chip_right = odd_tile()
    core_right = jnp.logical_not(chip_right)
    lane = lanes_of((ROWS, LANES))
    ground = surface[...]
    below = jnp.zeros((ROWS, LANES), F32)
    halo_from = by_side(core_right, 12, 0)
    is_halo = ((lane & 31) >= halo_from) & ((lane & 31) < halo_from + 6)
    halos = [from_core[0:32, :], from_core[32:64, :]]
    packed = None
    for level in reversed(range(OWN)):
        at = pl.ds(level * ROWS, ROWS)
        thermal = theta[at, :] * thickness[at, :] * SCALE
        fields = (ground + (below + 0.5 * thermal), wind[at, :])
        below = below + thermal
        out_p[at, :] = fields[0]
        here = slot(level)
        if level % 4 == 3:
            packed = [jnp.zeros((ROWS, LANES), F32)] * 4
        mine = (lane >= here) & (lane < here + 32)
        for i in range(2):
            for j, right in ((0, chip_right), (2, core_right)):
                side = swung(fields[i], right, here - 116, here + 6)
                if j == 2:
                    halo = swung(halos[i], right, here + 12 - 8 * level, here - 8 * level)
                    side = jnp.where(is_halo, halo, side)
                packed[i + j] = jnp.where(mine, side, packed[i + j])
        if level % 4 == 0:
            group = pl.ds(8 * level, ROWS)
            for ref, value in zip((chip_p, chip_w, core_p, core_w), packed):
                ref[group, :] = value
    p, w = substeps(out_p[...], wind[...])
    out_p[...] = p
    out_w[...] = w
    p, w = substeps(core_p[...], core_w[...])
    core_p[...] = p
    core_w[...] = w
    fix_edges(out_p, out_w, core_p, core_w, core_right, out_p, out_w, 0.0, 0.0)


def fix_edges(base_p, base_w, edge_p, edge_w, right, out_p, out_w, add_p, add_w):
    lane = lanes_of((ROWS, LANES))
    start = by_side(right, 122, 0)
    fixed = (lane >= start) & (lane < start + 6)
    for level in range(OWN):
        at = pl.ds(level * ROWS, ROWS)
        group = pl.ds(ROWS * (level // 4), ROWS)
        here = slot(level)
        for base, edge, out, add in (
            (base_p, edge_p, out_p, add_p),
            (base_w, edge_w, out_w, add_w),
        ):
            moved = swung(edge[group, :], right, 116 - here, -6 - here)
            out[at, :] = jnp.where(fixed, moved, base[at, :]) + add


def spread_heating(got, out_h, out_sum, rows_first):
    me = lax.axis_index("lev")
    beyond = jnp.zeros((8, LANES), F32)
    pieces = []
    for peer in range(PEERS):
        piece = got_parts(got, peer)
        pieces.append(piece)
        beyond = beyond + jnp.where(me < peer, 1.0, 0.0) * piece
    for group in range(4):
        out_sum[8 * group : 8 * group + 8, :] = jnp.where(
            top_half(), pieces[2 * group], halves_swapped(pieces[2 * group + 1])
        )
    out_sum[32:64, :] = unfolded(from_low_half(beyond))
    for peer in range(PEERS):
        rows_first[pl.ds(64 * peer, 64), :] = got[peer, 0:64, :].astype(F32)
    for level in range(OWN):
        out_h[pl.ds(level * ROWS, ROWS), :] = rows_first[pl.ds(level, ROWS, stride=OWN), :].astype(
            BF16
        )


def finish(from_chip, sums, local_p, local_w, chip_p, chip_w, out_p, out_w, edge_p, edge_w):
    right = odd_tile()
    lane = lanes_of((ROWS, LANES))
    halo_from = by_side(right, 12, 0)
    is_halo = ((lane & 31) >= halo_from) & ((lane & 31) < halo_from + 6)
    for base, edge, first in ((chip_p, edge_p, 0), (chip_w, edge_w, 32)):
        halos = from_chip[first : first + 32, :]
        for group in range(4):
            at = pl.ds(ROWS * group, ROWS)
            value = base[at, :]
            for level in range(4 * group, 4 * group + 4):
                here = slot(level)
                mine = is_halo & (lane >= here) & (lane < here + 32)
                halo = swung(halos, right, here + 12 - 8 * level, here - 8 * level)
                value = jnp.where(mine, halo, value)
            edge[at, :] = value
    p, w = substeps(edge_p[...], edge_w[...])
    edge_p[...] = p
    edge_w[...] = w
    main = sums[0:32, :]
    core = sums[32:64, :]
    chip = unfolded(from_chip[64:72, :])
    side = windowed(
        main, jnp.where(right, core, chip), turned(jnp.where(right, chip, core), 76)
    )
    zero = jnp.zeros((ROWS, LANES), F32)
    add_p, add_w = substeps(main, zero)
    side_p, side_w = substeps(side, zero)
    fix_edges(
        local_p, local_w, edge_p, edge_w, right, out_p, out_w, edges_in(add_p, side_p), edges_in(add_w, side_w)
    )


def call(kernel, outs, scratch=(), flops=100000, moved=1000000, room=8 << 20):
    return pl.pallas_call(
        kernel,
        out_shape=tuple(jax.ShapeDtypeStruct(s, d) for s, d in outs),
        scratch_shapes=[pltpu.VMEM(s, d) for s, d in scratch],
        compiler_params=pltpu.CompilerParams(vmem_limit_bytes=room),
        cost_estimate=pl.CostEstimate(flops=flops, bytes_accessed=moved, transcendentals=0),
    )


def coupled(theta, thickness, wind, surface, trigger, closure, closure_weights):
    flat = (OWN * ROWS, LANES)
    theta, thickness, wind = (x.reshape(flat) for x in (theta, thickness, wind))
    tiles = lax.axis_size("tile")
    (columns,) = call(send_columns, [((PEERS, PIECE, LANES), BF16)], room=60 << 20)(
        theta, thickness
    )
    columns = lax.all_to_all(columns, "lev", 0, 0, tiled=True)
    raw, to_core = call(send_borders, [((64, LANES), F32), ((72, LANES), F32)])(
        theta, thickness, wind, surface
    )
    between = [((t + 1) % tiles, (t + 2) % tiles) for t in range(0, tiles, 2)]
    within = [(t, t + 1) for t in range(0, tiles, 2)]
    from_core = lax.ppermute(to_core, "tile", within + [(b, a) for a, b in within])
    heats, to_chip = call(
        send_heating,
        [((PEERS, PIECE, LANES), BF16), ((72, LANES), F32)],
        [((512, 512), BF16)],
        flops=70000000,
    )(columns, trigger, closure, closure_weights, from_core, raw)
    heats = lax.all_to_all(heats, "lev", 0, 0, tiled=True)
    from_chip = lax.ppermute(to_chip, "tile", between + [(b, a) for a, b in between])
    packed = (4 * ROWS, LANES)
    local_p, local_w, chip_p, chip_w = call(
        local_substeps,
        [(flat, F32)] * 2 + [(packed, F32)] * 2,
        [(packed, F32)] * 2,
        flops=20000000,
    )(theta, thickness, wind, surface, from_core)
    heating, sums = call(
        spread_heating, [(flat, BF16), ((64, LANES), F32)], [(flat, F32)]
    )(heats)
    pressure, wind_next = call(finish, [(flat, F32)] * 2, [(packed, F32)] * 2)(
        from_chip, sums, local_p, local_w, chip_p, chip_w
    )
    shape = (OWN, ROWS, LANES)
    return pressure.reshape(shape), wind_next.reshape(shape), heating.reshape(shape)


def solution(mesh):
    in_specs = (
        P("lev", None, "tile"),
        P("lev", None, "tile"),
        P("lev", None, "tile"),
        P(None, "tile"),
        P(None, "tile"),
        P(None, "tile"),
        P(),
    )
    out_specs = (P("lev", None, "tile"), P("lev", None, "tile"), P("lev", None, "tile"))
    return jax.shard_map(
        coupled, mesh=mesh, in_specs=in_specs, out_specs=out_specs, check_vma=False
    )
```

```python
import jax
import jax.numpy as jnp
from jax import lax
from jax.experimental import pallas as pl
from jax.experimental.pallas import tpu as pltpu
from jax.sharding import PartitionSpec as P


LEVELS = 128
SUBSTEPS = 6
COURANT = 0.9
SCALE = LEVELS ** (-0.5)
PEERS = 8
OWN = 16
ROWS = 32
LANES = 128
BAND = 4
PIECE = 88
BF16 = jnp.bfloat16
F32 = jnp.float32


def lanes_of(shape):
    return lax.broadcasted_iota(jnp.int32, shape, len(shape) - 1)


def rows_of(shape):
    return lax.broadcasted_iota(jnp.int32, shape, len(shape) - 2)


def turned(x, shift):
    return pltpu.roll(x, shift % LANES, 1)


def three_parts(x):
    high = x.astype(BF16).astype(F32)
    rest = x - high
    middle = rest.astype(BF16).astype(F32)
    return high, middle, rest - middle


def sub(a, b):
    return a - COURANT * b


def substeps(pressure, wind):
    for _ in range(SUBSTEPS):
        wind = sub(wind, turned(pressure, -1) - pressure)
        pressure = sub(pressure, wind - turned(wind, 1))
    return pressure, wind


def short_chain(pressure, wind):
    for _ in range(SUBSTEPS):
        after, before = turned(pressure, -1), turned(pressure, 1)
        old = wind - turned(wind, 1)
        wind = sub(wind, after - pressure)
        change = old - COURANT * ((after - pressure) - (pressure - before))
        pressure = sub(pressure, change)
    return pressure, wind


def odd_tile():
    return lax.rem(lax.axis_index("tile"), 2) == 1


def by_side(right, if_right, if_left):
    return jnp.where(right, if_right % LANES, if_left % LANES)


def swung(x, right, if_right, if_left):
    return pltpu.roll(x, by_side(right, if_right, if_left), 1)


def folded(border):
    kept = jnp.where(lanes_of(border.shape) < 6, border, 0.0)
    out = kept[0:8]
    for group in range(1, 4):
        out = out + turned(kept[8 * group : 8 * group + 8], 8 * group)
    return out


def unfolded(fold):
    return jnp.concatenate([turned(fold, -8 * group) for group in range(4)])


def halves_swapped(x):
    return pltpu.roll(x, 4, 0)


def in_low_half(fold):
    return halves_swapped(fold) + turned(fold, 32)


def from_low_half(fold):
    top = rows_of(fold.shape) < 4
    return jnp.where(top, halves_swapped(fold), turned(fold, -32))


def top_half():
    return rows_of((8, LANES)) < 4


def send_parts(out, peer, x):
    high, middle, low = three_parts(x)
    out[peer, 64:80, :] = jnp.concatenate([high, middle]).astype(BF16)
    out[peer, 80:88, :] = low.astype(BF16)


def got_parts(got, peer):
    pair = got[peer, 64:80, :].astype(F32)
    return (pair[0:8] + pair[8:16]) + got[peer, 80:88, :].astype(F32)


def send_columns(theta, thickness, out):
    total = jnp.zeros((ROWS, LANES), F32)
    for level in range(OWN):
        at = pl.ds(level * ROWS, ROWS)
        total = total + theta[at, :] * thickness[at, :] * SCALE
    for row in range(ROWS):
        picked = theta[pl.ds(row, OWN, stride=ROWS), :]
        out[row // BAND, pl.ds(OWN * (row % BAND), OWN), :] = picked.astype(BF16)
    border = in_low_half(folded(swung(total, odd_tile(), -122, 0)))
    for group in range(4):
        rows = total[8 * group : 8 * group + 8]
        send_parts(out, 2 * group, jnp.where(top_half(), rows, border))
        send_parts(out, 2 * group + 1, jnp.where(top_half(), halves_swapped(rows), border))


def send_borders(theta, thickness, wind, surface, to_chip, to_core):
    lane = lanes_of((ROWS, LANES))
    zero = jnp.zeros((ROWS, LANES), F32)
    ground = surface[...]
    below = zero
    packed = [[zero, zero], [zero, zero]]
    for level in reversed(range(OWN)):
        at = pl.ds(level * ROWS, ROWS)
        thermal = theta[at, :] * thickness[at, :] * SCALE
        fields = (ground + (below + 0.5 * thermal), wind[at, :])
        below = below + thermal
        here = (lane >= 8 * level) & (lane < 8 * level + 8)
        for index, field in enumerate(fields):
            packed[0][index] = jnp.where(here, turned(field, 8 * level - 122), packed[0][index])
            packed[1][index] = jnp.where(here, turned(field, 8 * level), packed[1][index])
    odd = odd_tile()
    for index in range(2):
        at = pl.ds(ROWS * index, ROWS)
        to_chip[at, :] = jnp.where(odd, packed[0][index], packed[1][index])
        to_core[at, :] = jnp.where(odd, packed[1][index], packed[0][index])
    to_core[64:72, :] = folded(swung(below, odd, 0, -122))


def send_heating(got, trigger, closure, weights, from_core, raw, out, to_chip, stacked):
    me = lax.axis_index("lev")
    flags = trigger[pl.ds(BAND * me, BAND), :].astype(F32)
    scheme = closure[pl.ds(BAND * me, BAND), :]
    for row in range(BAND):
        chosen = [
            jnp.broadcast_to(
                jnp.where(scheme[row : row + 1] == s, flags[row : row + 1], 0.0), (OWN, LANES)
            ).astype(BF16)
            for s in range(3)
        ]
        columns = pl.ds(LANES * row, LANES)
        for peer in range(PEERS):
            block = got[peer, pl.ds(OWN * row, OWN), :]
            for s in range(3):
                stacked[pl.ds(LEVELS * s + OWN * peer, OWN), columns] = block * chosen[s]
            stacked[pl.ds(LEVELS * 3 + OWN * peer, OWN), columns] = block
    wide = jnp.concatenate([weights[s] for s in range(4)], axis=1)
    answer = jnp.dot(wide, stacked[...], preferred_element_type=F32).astype(BF16)
    for peer in range(PEERS):
        for row in range(BAND):
            out[peer, pl.ds(OWN * row, OWN), :] = answer[
                OWN * peer : OWN * peer + OWN, LANES * row : LANES * row + LANES
            ]
    core_border = in_low_half(from_core[64:72, :])
    higher = jnp.zeros((8, LANES), F32)
    beyond = jnp.zeros((8, LANES), F32)
    for peer in reversed(range(PEERS)):
        send_parts(out, peer, jnp.where(top_half(), higher, core_border))
        part = got_parts(got, peer)
        higher = higher + part
        beyond = beyond + jnp.where(me < peer, 1.0, 0.0) * part
    border = unfolded(from_low_half(beyond))
    border = jnp.where(lanes_of(border.shape) < 6, border, 0.0)
    for shift in (8, 16, 32, 64):
        border = border + turned(border, shift)
    to_chip[0:32, :] = raw[0:32, :] + border
    to_chip[32:64, :] = raw[32:64, :]


def slot(level):
    return 32 * (level % 4)


def halo_lanes(right):
    lane = lanes_of((ROWS, LANES)) & 31
    start = by_side(right, 12, 0)
    return (lane >= start) & (lane < start + 6)


def in_slot(level):
    lane = lanes_of((ROWS, LANES))
    return (lane >= slot(level)) & (lane < slot(level) + 32)


def band(level):
    return pl.ds(ROWS * (level // 4), ROWS)


def put_halos(base, halos, right, edge, extra):
    is_halo = halo_lanes(right)
    for first in range(0, OWN, 4):
        value = base[band(first), :]
        for level in range(first, first + 4):
            here = slot(level)
            halo = swung(halos, right, here + 12 - 8 * level, here - 8 * level)
            value = jnp.where(is_halo & in_slot(level), halo, value)
        edge[band(first), :] = value if extra is None else value + extra


def evolve(p, w):
    p[...], w[...] = short_chain(p[...], w[...])


def edge_lanes(right):
    lane = lanes_of((ROWS, LANES))
    start = by_side(right, 122, 0)
    return (lane >= start) & (lane < start + 6)


def edge_of(edge, level, right):
    return swung(edge[band(level), :], right, 116 - slot(level), -6 - slot(level))


def in_every_slot(field, right, if_right, if_left, kept):
    out = None
    for level in range(4):
        moved = swung(field, right, slot(level) + if_right, slot(level) + if_left)
        out = moved if out is None else jnp.where(in_slot(level), moved, out)
    return jnp.where(kept, out, 0.0)


def local_substeps(theta, thickness, wind, surface, out_p, out_w, chip_p, chip_w, core_p, core_w):
    chip_right = odd_tile()
    core_right = jnp.logical_not(chip_right)
    ground = surface[...]
    below = jnp.zeros((ROWS, LANES), F32)
    packed = None
    for level in reversed(range(OWN)):
        at = pl.ds(level * ROWS, ROWS)
        thermal = theta[at, :] * thickness[at, :] * SCALE
        fields = (ground + (below + 0.5 * thermal), wind[at, :])
        below = below + thermal
        out_p[at, :] = fields[0]
        here = slot(level)
        if level % 4 == 3:
            packed = [jnp.zeros((ROWS, LANES), F32)] * 4
        for i in range(2):
            for j, right in ((0, chip_right), (2, core_right)):
                side = swung(fields[i], right, here - 116, here + 6)
                packed[i + j] = jnp.where(in_slot(level), side, packed[i + j])
        if level % 4 == 0:
            for ref, value in zip((chip_p, chip_w, core_p, core_w), packed):
                ref[band(level), :] = value
    out_p[...], out_w[...] = substeps(out_p[...], wind[...])


def middle(
    got, from_core, local_p, local_w, chip_p, core_p, core_w, out_h, out_p, out_w, out_chip, edge_p, edge_w, rows_first
):
    me = lax.axis_index("lev")
    chip_right = odd_tile()
    core_right = jnp.logical_not(chip_right)
    beyond = jnp.zeros((8, LANES), F32)
    pieces = []
    for peer in range(PEERS):
        piece = got_parts(got, peer)
        pieces.append(piece)
        beyond = beyond + jnp.where(me < peer, 1.0, 0.0) * piece
    higher = jnp.concatenate(
        [
            jnp.where(top_half(), pieces[2 * group], halves_swapped(pieces[2 * group + 1]))
            for group in range(4)
        ]
    )
    border = unfolded(from_low_half(beyond))
    is_halo = halo_lanes(core_right)
    extra = in_every_slot(higher, core_right, -116, 6, jnp.logical_not(is_halo))
    extra = extra + in_every_slot(border, core_right, 12, 0, is_halo)
    put_halos(core_p, from_core[0:32, :], core_right, edge_p, extra)
    put_halos(core_w, from_core[32:64, :], core_right, edge_w, None)
    edge_p[128:160, :] = higher
    edge_w[128:160, :] = jnp.zeros((ROWS, LANES), F32)
    evolve(edge_p, edge_w)
    add_p = edge_p[128:160, :]
    add_w = edge_w[128:160, :]
    fixed = edge_lanes(core_right)
    for level in range(OWN):
        at = pl.ds(level * ROWS, ROWS)
        out_p[at, :] = jnp.where(fixed, edge_of(edge_p, level, core_right), local_p[at, :] + add_p)
        out_w[at, :] = jnp.where(fixed, edge_of(edge_w, level, core_right), local_w[at, :] + add_w)
    extra = in_every_slot(higher, chip_right, -116, 6, jnp.logical_not(halo_lanes(chip_right)))
    for first in range(0, OWN, 4):
        out_chip[band(first), :] = chip_p[band(first), :] + extra
    for peer in range(PEERS):
        rows_first[pl.ds(64 * peer, 64), :] = got[peer, 0:64, :].astype(F32)
    for level in range(OWN):
        out_h[pl.ds(level * ROWS, ROWS), :] = rows_first[pl.ds(level, ROWS, stride=OWN), :].astype(
            BF16
        )


def finish(
    from_chip, local_p, local_w, chip_p, chip_w, out_p, out_w, edge_p, edge_w, done_p, done_w, sems
):
    right = odd_tile()
    put_halos(chip_p, from_chip[0:32, :], right, edge_p, None)
    put_halos(chip_w, from_chip[32:64, :], right, edge_w, None)
    evolve(edge_p, edge_w)
    fixed = edge_lanes(right)
    copies = []
    for first in range(0, OWN, 4):
        for level in range(first, first + 4):
            at = pl.ds(level * ROWS, ROWS)
            done_p[at, :] = jnp.where(fixed, edge_of(edge_p, level, right), local_p[at, :])
            done_w[at, :] = jnp.where(fixed, edge_of(edge_w, level, right), local_w[at, :])
        block = pl.ds(first * ROWS, 4 * ROWS)
        for index, (done, out) in enumerate(((done_p, out_p), (done_w, out_w))):
            copy = pltpu.make_async_copy(
                done.at[block, :], out.at[block, :], sems.at[index, first // 4]
            )
            copy.start()
            copies.append(copy)
    for copy in copies:
        copy.wait()


def call(kernel, outs, scratch=(), flops=100000, moved=1000000, room=8 << 20, own_copies=False):
    held = [pltpu.VMEM(s, d) for s, d in scratch]
    more = {}
    if own_copies:
        held.append(pltpu.SemaphoreType.DMA((2, 4)))
        more = dict(out_specs=tuple(pl.BlockSpec(memory_space=pl.ANY) for _ in outs))
    return pl.pallas_call(
        kernel,
        out_shape=tuple(jax.ShapeDtypeStruct(s, d) for s, d in outs),
        scratch_shapes=held,
        compiler_params=pltpu.CompilerParams(vmem_limit_bytes=room),
        cost_estimate=pl.CostEstimate(flops=flops, bytes_accessed=moved, transcendentals=0),
        **more,
    )


def coupled(theta, thickness, wind, surface, trigger, closure, closure_weights):
    flat = (OWN * ROWS, LANES)
    theta, thickness, wind = (x.reshape(flat) for x in (theta, thickness, wind))
    tiles = lax.axis_size("tile")
    (columns,) = call(send_columns, [((PEERS, PIECE, LANES), BF16)], room=60 << 20)(
        theta, thickness
    )
    columns = lax.all_to_all(columns, "lev", 0, 0, tiled=True)
    raw, to_core = call(send_borders, [((64, LANES), F32), ((72, LANES), F32)])(
        theta, thickness, wind, surface
    )
    between = [((t + 1) % tiles, (t + 2) % tiles) for t in range(0, tiles, 2)]
    within = [(t, t + 1) for t in range(0, tiles, 2)]
    packed = (4 * ROWS, LANES)
    from_core = lax.ppermute(to_core, "tile", within + [(b, a) for a, b in within])
    local_p, local_w, chip_p, chip_w, core_p, core_w = call(
        local_substeps, [(flat, F32)] * 2 + [(packed, F32)] * 4, flops=20000000
    )(theta, thickness, wind, surface)
    heats, to_chip = call(
        send_heating,
        [((PEERS, PIECE, LANES), BF16), ((64, LANES), F32)],
        [((512, 512), BF16)],
        flops=70000000,
    )(columns, trigger, closure, closure_weights, from_core, raw)
    heats = lax.all_to_all(heats, "lev", 0, 0, tiled=True)
    from_chip = lax.ppermute(to_chip, "tile", between + [(b, a) for a, b in between])
    heating, local_p, local_w, chip_p = call(
        middle,
        [(flat, BF16), (flat, F32), (flat, F32), (packed, F32)],
        [((5 * ROWS, LANES), F32)] * 2 + [(flat, F32)],
    )(heats, from_core, local_p, local_w, chip_p, core_p, core_w)
    pressure, wind_next = call(
        finish, [(flat, F32)] * 2, [(packed, F32)] * 2 + [(flat, F32)] * 2, own_copies=True
    )(from_chip, local_p, local_w, chip_p, chip_w)
    shape = (OWN, ROWS, LANES)
    return pressure.reshape(shape), wind_next.reshape(shape), heating.reshape(shape)


def solution(mesh):
    in_specs = (
        P("lev", None, "tile"),
        P("lev", None, "tile"),
        P("lev", None, "tile"),
        P(None, "tile"),
        P(None, "tile"),
        P(None, "tile"),
        P(),
    )
    out_specs = (P("lev", None, "tile"), P("lev", None, "tile"), P("lev", None, "tile"))
    return jax.shard_map(
        coupled, mesh=mesh, in_specs=in_specs, out_specs=out_specs, check_vma=False
    )
```

```python
import jax
import jax.numpy as jnp
from jax import lax
from jax.experimental import pallas as pl
from jax.experimental.pallas import tpu as pltpu
from jax.sharding import PartitionSpec as P


LEVELS = 128
SUBSTEPS = 6
COURANT = 0.9
SCALE = LEVELS ** (-0.5)
PEERS = 8
OWN = 16
ROWS = 32
LANES = 128
BAND = 4
PIECE = 88
BF16 = jnp.bfloat16
F32 = jnp.float32


def lanes_of(shape):
    return lax.broadcasted_iota(jnp.int32, shape, len(shape) - 1)


def rows_of(shape):
    return lax.broadcasted_iota(jnp.int32, shape, len(shape) - 2)


def turned(x, shift):
    return pltpu.roll(x, shift % LANES, 1)


def three_parts(x):
    high = x.astype(BF16).astype(F32)
    rest = x - high
    middle = rest.astype(BF16).astype(F32)
    return high, middle, rest - middle


def sub(a, b):
    return a - COURANT * b


def substeps(pressure, wind):
    for _ in range(SUBSTEPS):
        after = turned(pressure, -1)
        before = turned(wind + COURANT * pressure, 1) - COURANT * pressure
        wind = sub(wind, after - pressure)
        pressure = sub(pressure, wind - before)
    return pressure, wind


def odd_tile():
    return lax.rem(lax.axis_index("tile"), 2) == 1


def by_side(right, if_right, if_left):
    return jnp.where(right, if_right % LANES, if_left % LANES)


def swung(x, right, if_right, if_left):
    return pltpu.roll(x, by_side(right, if_right, if_left), 1)


def folded(border):
    kept = jnp.where(lanes_of(border.shape) < 6, border, 0.0)
    out = kept[0:8]
    for group in range(1, 4):
        out = out + turned(kept[8 * group : 8 * group + 8], 8 * group)
    return out


def unfolded(fold):
    return jnp.concatenate([turned(fold, -8 * group) for group in range(4)])


def halves_swapped(x):
    return pltpu.roll(x, 4, 0)


def in_low_half(fold):
    return halves_swapped(fold) + turned(fold, 32)


def from_low_half(fold):
    top = rows_of(fold.shape) < 4
    return jnp.where(top, halves_swapped(fold), turned(fold, -32))


def top_half():
    return rows_of((8, LANES)) < 4


def send_parts(out, peer, x):
    high, middle, low = three_parts(x)
    out[peer, 64:80, :] = jnp.concatenate([high, middle]).astype(BF16)
    out[peer, 80:88, :] = low.astype(BF16)


def got_parts(got, peer):
    pair = got[peer, 64:80, :].astype(F32)
    return (pair[0:8] + pair[8:16]) + got[peer, 80:88, :].astype(F32)


def send_columns(theta, thickness, out):
    total = jnp.zeros((ROWS, LANES), F32)
    for level in range(OWN):
        at = pl.ds(level * ROWS, ROWS)
        total = total + theta[at, :] * thickness[at, :] * SCALE
    for row in range(ROWS):
        picked = theta[pl.ds(row, OWN, stride=ROWS), :]
        out[row // BAND, pl.ds(OWN * (row % BAND), OWN), :] = picked.astype(BF16)
    border = in_low_half(folded(swung(total, odd_tile(), -122, 0)))
    for group in range(4):
        rows = total[8 * group : 8 * group + 8]
        send_parts(out, 2 * group, jnp.where(top_half(), rows, border))
        send_parts(out, 2 * group + 1, jnp.where(top_half(), halves_swapped(rows), border))


def send_borders(theta, thickness, wind, surface, to_chip, to_core):
    lane = lanes_of((ROWS, LANES))
    zero = jnp.zeros((ROWS, LANES), F32)
    ground = surface[...]
    below = zero
    packed = [[zero, zero], [zero, zero]]
    for level in reversed(range(OWN)):
        at = pl.ds(level * ROWS, ROWS)
        thermal = theta[at, :] * thickness[at, :] * SCALE
        fields = (ground + (below + 0.5 * thermal), wind[at, :])
        below = below + thermal
        here = (lane >= 8 * level) & (lane < 8 * level + 8)
        for index, field in enumerate(fields):
            packed[0][index] = jnp.where(here, turned(field, 8 * level - 122), packed[0][index])
            packed[1][index] = jnp.where(here, turned(field, 8 * level), packed[1][index])
    odd = odd_tile()
    for index in range(2):
        at = pl.ds(ROWS * index, ROWS)
        to_chip[at, :] = jnp.where(odd, packed[0][index], packed[1][index])
        to_core[at, :] = jnp.where(odd, packed[1][index], packed[0][index])
    to_core[64:72, :] = folded(swung(below, odd, 0, -122))


def send_heating(got, trigger, closure, weights, from_core, raw, out, to_chip, stacked):
    me = lax.axis_index("lev")
    flags = trigger[pl.ds(BAND * me, BAND), :].astype(F32)
    scheme = closure[pl.ds(BAND * me, BAND), :]
    for row in range(BAND):
        chosen = [
            jnp.broadcast_to(
                jnp.where(scheme[row : row + 1] == s, flags[row : row + 1], 0.0), (OWN, LANES)
            ).astype(BF16)
            for s in range(3)
        ]
        columns = pl.ds(LANES * row, LANES)
        for peer in range(PEERS):
            block = got[peer, pl.ds(OWN * row, OWN), :]
            for s in range(3):
                stacked[pl.ds(LEVELS * s + OWN * peer, OWN), columns] = block * chosen[s]
            stacked[pl.ds(LEVELS * 3 + OWN * peer, OWN), columns] = block
    wide = jnp.concatenate([weights[s] for s in range(4)], axis=1)
    answer = jnp.dot(wide, stacked[...], preferred_element_type=F32).astype(BF16)
    for peer in range(PEERS):
        for row in range(BAND):
            out[peer, pl.ds(OWN * row, OWN), :] = answer[
                OWN * peer : OWN * peer + OWN, LANES * row : LANES * row + LANES
            ]
    core_border = in_low_half(from_core[64:72, :])
    higher = jnp.zeros((8, LANES), F32)
    beyond = jnp.zeros((8, LANES), F32)
    for peer in reversed(range(PEERS)):
        send_parts(out, peer, jnp.where(top_half(), higher, core_border))
        part = got_parts(got, peer)
        higher = higher + part
        beyond = beyond + jnp.where(me < peer, 1.0, 0.0) * part
    border = unfolded(from_low_half(beyond))
    border = jnp.where(lanes_of(border.shape) < 6, border, 0.0)
    for shift in (8, 16, 32, 64):
        border = border + turned(border, shift)
    to_chip[0:32, :] = raw[0:32, :] + border
    to_chip[32:64, :] = raw[32:64, :]


def slot(level):
    return 32 * (level % 4)


def halo_lanes(right):
    lane = lanes_of((ROWS, LANES)) & 31
    start = by_side(right, 12, 0)
    return (lane >= start) & (lane < start + 6)


def in_slot(level):
    lane = lanes_of((ROWS, LANES))
    return (lane >= slot(level)) & (lane < slot(level) + 32)


def band(level):
    return pl.ds(ROWS * (level // 4), ROWS)


def put_halos(base, halos, right, edge, extra):
    is_halo = halo_lanes(right)
    for first in range(0, OWN, 4):
        value = base[band(first), :]
        for level in range(first, first + 4):
            here = slot(level)
            halo = swung(halos, right, here + 12 - 8 * level, here - 8 * level)
            value = jnp.where(is_halo & in_slot(level), halo, value)
        edge[band(first), :] = value if extra is None else value + extra


def evolve(p, w):
    p[...], w[...] = substeps(p[...], w[...])


def edge_lanes(right):
    lane = lanes_of((ROWS, LANES))
    start = by_side(right, 122, 0)
    return (lane >= start) & (lane < start + 6)


def edge_of(edge, level, right):
    return swung(edge[band(level), :], right, 116 - slot(level), -6 - slot(level))


def in_every_slot(field, right, if_right, if_left, kept):
    out = None
    for level in range(4):
        moved = swung(field, right, slot(level) + if_right, slot(level) + if_left)
        out = moved if out is None else jnp.where(in_slot(level), moved, out)
    return jnp.where(kept, out, 0.0)


def local_substeps(theta, thickness, wind, surface, out_p, out_w, chip_p, chip_w, core_p, core_w):
    chip_right = odd_tile()
    core_right = jnp.logical_not(chip_right)
    ground = surface[...]
    below = jnp.zeros((ROWS, LANES), F32)
    packed = None
    for level in reversed(range(OWN)):
        at = pl.ds(level * ROWS, ROWS)
        thermal = theta[at, :] * thickness[at, :] * SCALE
        fields = (ground + (below + 0.5 * thermal), wind[at, :])
        below = below + thermal
        out_p[at, :] = fields[0]
        here = slot(level)
        if level % 4 == 3:
            packed = [jnp.zeros((ROWS, LANES), F32)] * 4
        for i in range(2):
            for j, right in ((0, chip_right), (2, core_right)):
                side = swung(fields[i], right, here - 116, here + 6)
                packed[i + j] = jnp.where(in_slot(level), side, packed[i + j])
        if level % 4 == 0:
            for ref, value in zip((chip_p, chip_w, core_p, core_w), packed):
                ref[band(level), :] = value
    out_p[...], out_w[...] = substeps(out_p[...], wind[...])


def middle(
    got, from_core, local_p, local_w, chip_p, core_p, core_w, out_h, out_p, out_w, out_chip, edge_p, edge_w, rows_first
):
    me = lax.axis_index("lev")
    chip_right = odd_tile()
    core_right = jnp.logical_not(chip_right)
    beyond = jnp.zeros((8, LANES), F32)
    pieces = []
    for peer in range(PEERS):
        piece = got_parts(got, peer)
        pieces.append(piece)
        beyond = beyond + jnp.where(me < peer, 1.0, 0.0) * piece
    higher = jnp.concatenate(
        [
            jnp.where(top_half(), pieces[2 * group], halves_swapped(pieces[2 * group + 1]))
            for group in range(4)
        ]
    )
    border = unfolded(from_low_half(beyond))
    is_halo = halo_lanes(core_right)
    extra = in_every_slot(higher, core_right, -116, 6, jnp.logical_not(is_halo))
    extra = extra + in_every_slot(border, core_right, 12, 0, is_halo)
    put_halos(core_p, from_core[0:32, :], core_right, edge_p, extra)
    put_halos(core_w, from_core[32:64, :], core_right, edge_w, None)
    edge_p[128:160, :] = higher
    edge_w[128:160, :] = jnp.zeros((ROWS, LANES), F32)
    evolve(edge_p, edge_w)
    add_p = edge_p[128:160, :]
    add_w = edge_w[128:160, :]
    fixed = edge_lanes(core_right)
    for level in range(OWN):
        at = pl.ds(level * ROWS, ROWS)
        out_p[at, :] = jnp.where(fixed, edge_of(edge_p, level, core_right), local_p[at, :] + add_p)
        out_w[at, :] = jnp.where(fixed, edge_of(edge_w, level, core_right), local_w[at, :] + add_w)
    extra = in_every_slot(higher, chip_right, -116, 6, jnp.logical_not(halo_lanes(chip_right)))
    for first in range(0, OWN, 4):
        out_chip[band(first), :] = chip_p[band(first), :] + extra
    for peer in range(PEERS):
        rows_first[pl.ds(64 * peer, 64), :] = got[peer, 0:64, :].astype(F32)
    for level in range(OWN):
        out_h[pl.ds(level * ROWS, ROWS), :] = rows_first[pl.ds(level, ROWS, stride=OWN), :].astype(
            BF16
        )


def finish(
    from_chip, heating, local_p, local_w, chip_p, chip_w, out_p, out_w, out_h, edge_p, edge_w, done_p, done_w, sems
):
    copies = [pltpu.make_async_copy(heating, out_h, sems.at[8])]
    copies[0].start()
    right = odd_tile()
    put_halos(chip_p, from_chip[0:32, :], right, edge_p, None)
    put_halos(chip_w, from_chip[32:64, :], right, edge_w, None)
    evolve(edge_p, edge_w)
    fixed = edge_lanes(right)
    for first in range(0, OWN, 4):
        for level in range(first, first + 4):
            at = pl.ds(level * ROWS, ROWS)
            done_p[at, :] = jnp.where(fixed, edge_of(edge_p, level, right), local_p[at, :])
            done_w[at, :] = jnp.where(fixed, edge_of(edge_w, level, right), local_w[at, :])
        block = pl.ds(first * ROWS, 4 * ROWS)
        for index, (done, out) in enumerate(((done_p, out_p), (done_w, out_w))):
            copy = pltpu.make_async_copy(
                done.at[block, :], out.at[block, :], sems.at[4 * index + first // 4]
            )
            copy.start()
            copies.append(copy)
    for copy in copies:
        copy.wait()


def call(kernel, outs, scratch=(), flops=100000, moved=1000000, room=8 << 20, own_copies=False):
    held = [pltpu.VMEM(s, d) for s, d in scratch]
    more = {}
    if own_copies:
        held.append(pltpu.SemaphoreType.DMA((9,)))
        more = dict(out_specs=tuple(pl.BlockSpec(memory_space=pl.ANY) for _ in outs))
    return pl.pallas_call(
        kernel,
        out_shape=tuple(jax.ShapeDtypeStruct(s, d) for s, d in outs),
        scratch_shapes=held,
        compiler_params=pltpu.CompilerParams(vmem_limit_bytes=room),
        cost_estimate=pl.CostEstimate(flops=flops, bytes_accessed=moved, transcendentals=0),
        **more,
    )


def coupled(theta, thickness, wind, surface, trigger, closure, closure_weights):
    flat = (OWN * ROWS, LANES)
    theta, thickness, wind = (x.reshape(flat) for x in (theta, thickness, wind))
    tiles = lax.axis_size("tile")
    (columns,) = call(send_columns, [((PEERS, PIECE, LANES), BF16)], room=60 << 20)(
        theta, thickness
    )
    columns = lax.all_to_all(columns, "lev", 0, 0, tiled=True)
    raw, to_core = call(send_borders, [((64, LANES), F32), ((72, LANES), F32)])(
        theta, thickness, wind, surface
    )
    between = [((t + 1) % tiles, (t + 2) % tiles) for t in range(0, tiles, 2)]
    within = [(t, t + 1) for t in range(0, tiles, 2)]
    packed = (4 * ROWS, LANES)
    from_core = lax.ppermute(to_core, "tile", within + [(b, a) for a, b in within])
    local_p, local_w, chip_p, chip_w, core_p, core_w = call(
        local_substeps, [(flat, F32)] * 2 + [(packed, F32)] * 4, flops=20000000
    )(theta, thickness, wind, surface)
    heats, to_chip = call(
        send_heating,
        [((PEERS, PIECE, LANES), BF16), ((64, LANES), F32)],
        [((512, 512), BF16)],
        flops=70000000,
    )(columns, trigger, closure, closure_weights, from_core, raw)
    heats = lax.all_to_all(heats, "lev", 0, 0, tiled=True)
    from_chip = lax.ppermute(to_chip, "tile", between + [(b, a) for a, b in between])
    heating, local_p, local_w, chip_p = call(
        middle,
        [(flat, BF16), (flat, F32), (flat, F32), (packed, F32)],
        [((5 * ROWS, LANES), F32)] * 2 + [(flat, F32)],
    )(heats, from_core, local_p, local_w, chip_p, core_p, core_w)
    pressure, wind_next, heating = call(
        finish,
        [(flat, F32), (flat, F32), (flat, BF16)],
        [(packed, F32)] * 2 + [(flat, F32)] * 2,
        own_copies=True,
    )(from_chip, heating, local_p, local_w, chip_p, chip_w)
    shape = (OWN, ROWS, LANES)
    return pressure.reshape(shape), wind_next.reshape(shape), heating.reshape(shape)


def solution(mesh):
    in_specs = (
        P("lev", None, "tile"),
        P("lev", None, "tile"),
        P("lev", None, "tile"),
        P(None, "tile"),
        P(None, "tile"),
        P(None, "tile"),
        P(),
    )
    out_specs = (P("lev", None, "tile"), P("lev", None, "tile"), P("lev", None, "tile"))
    return jax.shard_map(
        coupled, mesh=mesh, in_specs=in_specs, out_specs=out_specs, check_vma=False
    )
```

```python
import jax
import jax.numpy as jnp
from jax import lax
from jax.experimental import pallas as pl
from jax.experimental.pallas import tpu as pltpu
from jax.sharding import PartitionSpec as P


LEVELS = 128
SUBSTEPS = 6
COURANT = 0.9
SCALE = LEVELS ** (-0.5)
PEERS = 8
OWN = 16
ROWS = 32
LANES = 128
BAND = 4
PIECE = 88
BF16 = jnp.bfloat16
F32 = jnp.float32


def lanes_of(shape):
    return lax.broadcasted_iota(jnp.int32, shape, len(shape) - 1)


def rows_of(shape):
    return lax.broadcasted_iota(jnp.int32, shape, len(shape) - 2)


def turned(x, shift):
    return pltpu.roll(x, shift % LANES, 1)


def three_parts(x):
    high = x.astype(BF16).astype(F32)
    rest = x - high
    middle = rest.astype(BF16).astype(F32)
    return high, middle, rest - middle


def sub(a, b):
    return a - COURANT * b


def substeps(pressure, wind):
    for _ in range(SUBSTEPS):
        after = turned(pressure, -1)
        before = turned(wind + COURANT * pressure, 1) - COURANT * pressure
        wind = sub(wind, after - pressure)
        pressure = sub(pressure, wind - before)
    return pressure, wind


def odd_tile():
    return lax.rem(lax.axis_index("tile"), 2) == 1


def by_side(right, if_right, if_left):
    return jnp.where(right, if_right % LANES, if_left % LANES)


def swung(x, right, if_right, if_left):
    return pltpu.roll(x, by_side(right, if_right, if_left), 1)


def folded(border):
    kept = jnp.where(lanes_of(border.shape) < 6, border, 0.0)
    out = kept[0:8]
    for group in range(1, 4):
        out = out + turned(kept[8 * group : 8 * group + 8], 8 * group)
    return out


def unfolded(fold):
    return jnp.concatenate([turned(fold, -8 * group) for group in range(4)])


def halves_swapped(x):
    return pltpu.roll(x, 4, 0)


def in_low_half(fold):
    return halves_swapped(fold) + turned(fold, 32)


def from_low_half(fold):
    top = rows_of(fold.shape) < 4
    return jnp.where(top, halves_swapped(fold), turned(fold, -32))


def top_half():
    return rows_of((8, LANES)) < 4


def send_parts(out, peer, x):
    high, middle, low = three_parts(x)
    out[peer, 64:80, :] = jnp.concatenate([high, middle]).astype(BF16)
    out[peer, 80:88, :] = low.astype(BF16)


def got_parts(got, peer):
    pair = got[peer, 64:80, :].astype(F32)
    return (pair[0:8] + pair[8:16]) + got[peer, 80:88, :].astype(F32)


def in_two_rows(fold):
    rows = [turned(pltpu.roll(fold, 8 - 2 * pair, 0), 32 * pair) for pair in range(1, 4)]
    return ((fold + rows[0]) + rows[1]) + rows[2]


def from_two_rows(packed):
    row = rows_of(packed.shape)
    out = packed
    for pair in range(1, 4):
        out = jnp.where(
            row >= 2 * pair, turned(pltpu.roll(packed, 2 * pair, 0), -32 * pair), out
        )
    return out


def send_columns(theta, thickness, out):
    total = jnp.zeros((ROWS, LANES), F32)
    for level in range(OWN):
        at = pl.ds(level * ROWS, ROWS)
        total = total + theta[at, :] * thickness[at, :] * SCALE
    for row in range(ROWS):
        picked = theta[pl.ds(row, OWN, stride=ROWS), :]
        out[row // BAND, pl.ds(OWN * (row % BAND), OWN), :] = picked.astype(BF16)
    high, middle, _ = three_parts(in_two_rows(folded(swung(total, odd_tile(), -122, 0))))
    row = rows_of((8, LANES))
    border = jnp.where(row < 6, halves_swapped(high), pltpu.roll(middle, 6, 0))
    for group in range(4):
        parts = three_parts(total[8 * group : 8 * group + 8])
        for side in range(2):
            same = [p if side == 0 else halves_swapped(p) for p in parts]
            first = jnp.where(top_half(), same[0], halves_swapped(same[1]))
            second = jnp.where(top_half(), same[2], border)
            out[2 * group + side, 64:80, :] = jnp.concatenate([first, second]).astype(BF16)


def send_borders(theta, thickness, wind, surface, to_chip, to_core):
    lane = lanes_of((ROWS, LANES))
    zero = jnp.zeros((ROWS, LANES), F32)
    ground = surface[...]
    below = zero
    packed = [[zero, zero], [zero, zero]]
    for level in reversed(range(OWN)):
        at = pl.ds(level * ROWS, ROWS)
        thermal = theta[at, :] * thickness[at, :] * SCALE
        fields = (ground + (below + 0.5 * thermal), wind[at, :])
        below = below + thermal
        here = (lane >= 8 * level) & (lane < 8 * level + 8)
        for index, field in enumerate(fields):
            packed[0][index] = jnp.where(here, turned(field, 8 * level - 122), packed[0][index])
            packed[1][index] = jnp.where(here, turned(field, 8 * level), packed[1][index])
    odd = odd_tile()
    for index in range(2):
        at = pl.ds(ROWS * index, ROWS)
        to_chip[at, :] = jnp.where(odd, packed[0][index], packed[1][index])
        to_core[at, :] = jnp.where(odd, packed[1][index], packed[0][index])
    to_core[64:72, :] = folded(swung(below, odd, 0, -122))


def send_heating(got, trigger, closure, weights, from_core, raw, out, to_chip, stacked):
    me = lax.axis_index("lev")
    flags = trigger[pl.ds(BAND * me, BAND), :].astype(F32)
    scheme = closure[pl.ds(BAND * me, BAND), :]
    for row in range(BAND):
        chosen = [
            jnp.broadcast_to(
                jnp.where(scheme[row : row + 1] == s, flags[row : row + 1], 0.0), (OWN, LANES)
            ).astype(BF16)
            for s in range(3)
        ]
        columns = pl.ds(LANES * row, LANES)
        for peer in range(PEERS):
            block = got[peer, pl.ds(OWN * row, OWN), :]
            for s in range(3):
                stacked[pl.ds(LEVELS * s + OWN * peer, OWN), columns] = block * chosen[s]
            stacked[pl.ds(LEVELS * 3 + OWN * peer, OWN), columns] = block
    wide = jnp.concatenate([weights[s] for s in range(4)], axis=1)
    answer = jnp.dot(wide, stacked[...], preferred_element_type=F32).astype(BF16)
    for peer in range(PEERS):
        for row in range(BAND):
            out[peer, pl.ds(OWN * row, OWN), :] = answer[
                OWN * peer : OWN * peer + OWN, LANES * row : LANES * row + LANES
            ]
    core_border = in_low_half(from_core[64:72, :])
    higher = jnp.zeros((8, LANES), F32)
    beyond = jnp.zeros((8, LANES), F32)
    for peer in reversed(range(PEERS)):
        send_parts(out, peer, jnp.where(top_half(), higher, core_border))
        pair = got[peer, 64:80, :].astype(F32)
        higher = higher + ((pair[0:8] + halves_swapped(pair[0:8])) + pair[8:16])
        part = halves_swapped(pair[8:16]) + pltpu.roll(pair[8:16], 2, 0)
        beyond = beyond + jnp.where(me < peer, 1.0, 0.0) * part
    border = unfolded(from_two_rows(beyond))
    border = jnp.where(lanes_of(border.shape) < 6, border, 0.0)
    for shift in (8, 16, 32, 64):
        border = border + turned(border, shift)
    to_chip[0:32, :] = raw[0:32, :] + border
    to_chip[32:64, :] = raw[32:64, :]


def slot(level):
    return 32 * (level % 4)


def halo_lanes(right):
    lane = lanes_of((ROWS, LANES)) & 31
    start = by_side(right, 12, 0)
    return (lane >= start) & (lane < start + 6)


def in_slot(level):
    lane = lanes_of((ROWS, LANES))
    return (lane >= slot(level)) & (lane < slot(level) + 32)


def band(level):
    return pl.ds(ROWS * (level // 4), ROWS)


def put_halos(base, halos, right, edge, extra):
    is_halo = halo_lanes(right)
    for first in range(0, OWN, 4):
        value = base[band(first), :]
        for level in range(first, first + 4):
            here = slot(level)
            halo = swung(halos, right, here + 12 - 8 * level, here - 8 * level)
            value = jnp.where(is_halo & in_slot(level), halo, value)
        edge[band(first), :] = value if extra is None else value + extra


def evolve(p, w):
    p[...], w[...] = substeps(p[...], w[...])


def edge_lanes(right):
    lane = lanes_of((ROWS, LANES))
    start = by_side(right, 122, 0)
    return (lane >= start) & (lane < start + 6)


def edge_of(edge, level, right):
    return swung(edge[band(level), :], right, 116 - slot(level), -6 - slot(level))


def in_every_slot(field, right, if_right, if_left, kept):
    out = None
    for level in range(4):
        moved = swung(field, right, slot(level) + if_right, slot(level) + if_left)
        out = moved if out is None else jnp.where(in_slot(level), moved, out)
    return jnp.where(kept, out, 0.0)


def local_substeps(theta, thickness, wind, surface, out_p, out_w, chip_p, chip_w, core_p, core_w):
    chip_right = odd_tile()
    core_right = jnp.logical_not(chip_right)
    ground = surface[...]
    below = jnp.zeros((ROWS, LANES), F32)
    packed = None
    for level in reversed(range(OWN)):
        at = pl.ds(level * ROWS, ROWS)
        thermal = theta[at, :] * thickness[at, :] * SCALE
        fields = (ground + (below + 0.5 * thermal), wind[at, :])
        below = below + thermal
        out_p[at, :] = fields[0]
        here = slot(level)
        if level % 4 == 3:
            packed = [jnp.zeros((ROWS, LANES), F32)] * 4
        for i in range(2):
            for j, right in ((0, chip_right), (2, core_right)):
                side = swung(fields[i], right, here - 116, here + 6)
                packed[i + j] = jnp.where(in_slot(level), side, packed[i + j])
        if level % 4 == 0:
            for ref, value in zip((chip_p, chip_w, core_p, core_w), packed):
                ref[band(level), :] = value
    out_p[...], out_w[...] = substeps(out_p[...], wind[...])


def middle(
    got, from_core, local_p, local_w, chip_p, core_p, core_w, out_h, out_p, out_w, out_chip, edge_p, edge_w, rows_first
):
    me = lax.axis_index("lev")
    chip_right = odd_tile()
    core_right = jnp.logical_not(chip_right)
    beyond = jnp.zeros((8, LANES), F32)
    pieces = []
    for peer in range(PEERS):
        piece = got_parts(got, peer)
        pieces.append(piece)
        beyond = beyond + jnp.where(me < peer, 1.0, 0.0) * piece
    higher = jnp.concatenate(
        [
            jnp.where(top_half(), pieces[2 * group], halves_swapped(pieces[2 * group + 1]))
            for group in range(4)
        ]
    )
    border = unfolded(from_low_half(beyond))
    is_halo = halo_lanes(core_right)
    extra = in_every_slot(higher, core_right, -116, 6, jnp.logical_not(is_halo))
    extra = extra + in_every_slot(border, core_right, 12, 0, is_halo)
    put_halos(core_p, from_core[0:32, :], core_right, edge_p, extra)
    put_halos(core_w, from_core[32:64, :], core_right, edge_w, None)
    edge_p[128:160, :] = higher
    edge_w[128:160, :] = jnp.zeros((ROWS, LANES), F32)
    evolve(edge_p, edge_w)
    add_p = edge_p[128:160, :]
    add_w = edge_w[128:160, :]
    fixed = edge_lanes(core_right)
    for level in range(OWN):
        at = pl.ds(level * ROWS, ROWS)
        out_p[at, :] = jnp.where(fixed, edge_of(edge_p, level, core_right), local_p[at, :] + add_p)
        out_w[at, :] = jnp.where(fixed, edge_of(edge_w, level, core_right), local_w[at, :] + add_w)
    extra = in_every_slot(higher, chip_right, -116, 6, jnp.logical_not(halo_lanes(chip_right)))
    for first in range(0, OWN, 4):
        out_chip[band(first), :] = chip_p[band(first), :] + extra
    for peer in range(PEERS):
        rows_first[pl.ds(64 * peer, 64), :] = got[peer, 0:64, :].astype(F32)
    for level in range(OWN):
        out_h[pl.ds(level * ROWS, ROWS), :] = rows_first[pl.ds(level, ROWS, stride=OWN), :].astype(
            BF16
        )


def finish(
    from_chip, heating, local_p, local_w, chip_p, chip_w, out_p, out_w, out_h, edge_p, edge_w, done_p, done_w, sems
):
    copies = [pltpu.make_async_copy(heating, out_h, sems.at[8])]
    copies[0].start()
    right = odd_tile()
    put_halos(chip_p, from_chip[0:32, :], right, edge_p, None)
    put_halos(chip_w, from_chip[32:64, :], right, edge_w, None)
    evolve(edge_p, edge_w)
    fixed = edge_lanes(right)
    for first in range(0, OWN, 4):
        for level in range(first, first + 4):
            at = pl.ds(level * ROWS, ROWS)
            done_p[at, :] = jnp.where(fixed, edge_of(edge_p, level, right), local_p[at, :])
            done_w[at, :] = jnp.where(fixed, edge_of(edge_w, level, right), local_w[at, :])
        block = pl.ds(first * ROWS, 4 * ROWS)
        for index, (done, out) in enumerate(((done_p, out_p), (done_w, out_w))):
            copy = pltpu.make_async_copy(
                done.at[block, :], out.at[block, :], sems.at[4 * index + first // 4]
            )
            copy.start()
            copies.append(copy)
    for copy in copies:
        copy.wait()


def call(kernel, outs, scratch=(), flops=100000, moved=1000000, room=8 << 20, own_copies=False):
    held = [pltpu.VMEM(s, d) for s, d in scratch]
    more = {}
    if own_copies:
        held.append(pltpu.SemaphoreType.DMA((9,)))
        more = dict(out_specs=tuple(pl.BlockSpec(memory_space=pl.ANY) for _ in outs))
    return pl.pallas_call(
        kernel,
        out_shape=tuple(jax.ShapeDtypeStruct(s, d) for s, d in outs),
        scratch_shapes=held,
        compiler_params=pltpu.CompilerParams(vmem_limit_bytes=room),
        cost_estimate=pl.CostEstimate(flops=flops, bytes_accessed=moved, transcendentals=0),
        **more,
    )


def coupled(theta, thickness, wind, surface, trigger, closure, closure_weights):
    flat = (OWN * ROWS, LANES)
    theta, thickness, wind = (x.reshape(flat) for x in (theta, thickness, wind))
    tiles = lax.axis_size("tile")
    (columns,) = call(send_columns, [((PEERS, 80, LANES), BF16)], room=60 << 20)(
        theta, thickness
    )
    columns = lax.all_to_all(columns, "lev", 0, 0, tiled=True)
    raw, to_core = call(send_borders, [((64, LANES), F32), ((72, LANES), F32)])(
        theta, thickness, wind, surface
    )
    between = [((t + 1) % tiles, (t + 2) % tiles) for t in range(0, tiles, 2)]
    within = [(t, t + 1) for t in range(0, tiles, 2)]
    packed = (4 * ROWS, LANES)
    from_core = lax.ppermute(to_core, "tile", within + [(b, a) for a, b in within])
    local_p, local_w, chip_p, chip_w, core_p, core_w = call(
        local_substeps, [(flat, F32)] * 2 + [(packed, F32)] * 4, flops=20000000
    )(theta, thickness, wind, surface)
    heats, to_chip = call(
        send_heating,
        [((PEERS, PIECE, LANES), BF16), ((64, LANES), F32)],
        [((512, 512), BF16)],
        flops=70000000,
    )(columns, trigger, closure, closure_weights, from_core, raw)
    heats = lax.all_to_all(heats, "lev", 0, 0, tiled=True)
    from_chip = lax.ppermute(to_chip, "tile", between + [(b, a) for a, b in between])
    heating, local_p, local_w, chip_p = call(
        middle,
        [(flat, BF16), (flat, F32), (flat, F32), (packed, F32)],
        [((5 * ROWS, LANES), F32)] * 2 + [(flat, F32)],
    )(heats, from_core, local_p, local_w, chip_p, core_p, core_w)
    pressure, wind_next, heating = call(
        finish,
        [(flat, F32), (flat, F32), (flat, BF16)],
        [(packed, F32)] * 2 + [(flat, F32)] * 2,
        own_copies=True,
    )(from_chip, heating, local_p, local_w, chip_p, chip_w)
    shape = (OWN, ROWS, LANES)
    return pressure.reshape(shape), wind_next.reshape(shape), heating.reshape(shape)


def solution(mesh):
    in_specs = (
        P("lev", None, "tile"),
        P("lev", None, "tile"),
        P("lev", None, "tile"),
        P(None, "tile"),
        P(None, "tile"),
        P(None, "tile"),
        P(),
    )
    out_specs = (P("lev", None, "tile"), P("lev", None, "tile"), P("lev", None, "tile"))
    return jax.shard_map(
        coupled, mesh=mesh, in_specs=in_specs, out_specs=out_specs, check_vma=False
    )
```

```python
import jax
import jax.numpy as jnp
from jax import lax
from jax.experimental import pallas as pl
from jax.experimental.pallas import tpu as pltpu
from jax.sharding import PartitionSpec as P


LEVELS = 128
SUBSTEPS = 6
COURANT = 0.9
SCALE = LEVELS ** (-0.5)
PEERS = 8
OWN = 16
ROWS = 32
LANES = 128
BAND = 4
PIECE = 88
BF16 = jnp.bfloat16
F32 = jnp.float32


def lanes_of(shape):
    return lax.broadcasted_iota(jnp.int32, shape, len(shape) - 1)


def rows_of(shape):
    return lax.broadcasted_iota(jnp.int32, shape, len(shape) - 2)


def turned(x, shift):
    return pltpu.roll(x, shift % LANES, 1)


def three_parts(x):
    high = x.astype(BF16).astype(F32)
    rest = x - high
    middle = rest.astype(BF16).astype(F32)
    return high, middle, rest - middle


def sub(a, b):
    return a - COURANT * b


def substeps(pressure, wind):
    for _ in range(SUBSTEPS):
        after = turned(pressure, -1)
        before = turned(wind + COURANT * pressure, 1) - COURANT * pressure
        wind = sub(wind, after - pressure)
        pressure = sub(pressure, wind - before)
    return pressure, wind


def odd_tile():
    return lax.rem(lax.axis_index("tile"), 2) == 1


def by_side(right, if_right, if_left):
    return jnp.where(right, if_right % LANES, if_left % LANES)


def swung(x, right, if_right, if_left):
    return pltpu.roll(x, by_side(right, if_right, if_left), 1)


def folded(border):
    kept = jnp.where(lanes_of(border.shape) < 6, border, 0.0)
    out = kept[0:8]
    for group in range(1, 4):
        out = out + turned(kept[8 * group : 8 * group + 8], 8 * group)
    return out


def unfolded(fold):
    return jnp.concatenate([turned(fold, -8 * group) for group in range(4)])


def halves_swapped(x):
    return pltpu.roll(x, 4, 0)


def in_low_half(fold):
    return halves_swapped(fold) + turned(fold, 32)


def from_low_half(fold):
    top = rows_of(fold.shape) < 4
    return jnp.where(top, halves_swapped(fold), turned(fold, -32))


def top_half():
    return rows_of((8, LANES)) < 4


def send_parts(out, peer, x):
    high, middle, low = three_parts(x)
    out[peer, 64:80, :] = jnp.concatenate([high, middle]).astype(BF16)
    out[peer, 80:88, :] = low.astype(BF16)


def got_parts(got, peer):
    pair = got[peer, 64:80, :].astype(F32)
    return (pair[0:8] + pair[8:16]) + got[peer, 80:88, :].astype(F32)


def in_two_rows(fold):
    rows = [turned(pltpu.roll(fold, 8 - 2 * pair, 0), 32 * pair) for pair in range(1, 4)]
    return ((fold + rows[0]) + rows[1]) + rows[2]


def from_two_rows(packed):
    row = rows_of(packed.shape)
    out = packed
    for pair in range(1, 4):
        out = jnp.where(
            row >= 2 * pair, turned(pltpu.roll(packed, 2 * pair, 0), -32 * pair), out
        )
    return out


def send_columns(theta, thickness, out):
    total = jnp.zeros((ROWS, LANES), F32)
    for level in range(OWN):
        at = pl.ds(level * ROWS, ROWS)
        total = total + theta[at, :] * thickness[at, :] * SCALE
    for row in range(ROWS):
        picked = theta[pl.ds(row, OWN, stride=ROWS), :]
        out[row // BAND, pl.ds(OWN * (row % BAND), OWN), :] = picked.astype(BF16)
    high, middle, _ = three_parts(in_two_rows(folded(swung(total, odd_tile(), -122, 0))))
    row = rows_of((8, LANES))
    border = jnp.where(row < 6, halves_swapped(high), pltpu.roll(middle, 6, 0))
    for group in range(4):
        parts = three_parts(total[8 * group : 8 * group + 8])
        for side in range(2):
            same = [p if side == 0 else halves_swapped(p) for p in parts]
            first = jnp.where(top_half(), same[0], halves_swapped(same[1]))
            second = jnp.where(top_half(), same[2], border)
            out[2 * group + side, 64:80, :] = jnp.concatenate([first, second]).astype(BF16)


def send_borders(theta, thickness, wind, surface, to_chip, to_core):
    lane = lanes_of((ROWS, LANES))
    zero = jnp.zeros((ROWS, LANES), F32)
    ground = surface[...]
    below = zero
    packed = [[zero, zero], [zero, zero]]
    for level in reversed(range(OWN)):
        at = pl.ds(level * ROWS, ROWS)
        thermal = theta[at, :] * thickness[at, :] * SCALE
        fields = (ground + (below + 0.5 * thermal), wind[at, :])
        below = below + thermal
        here = (lane >= 8 * level) & (lane < 8 * level + 8)
        for index, field in enumerate(fields):
            packed[0][index] = jnp.where(here, turned(field, 8 * level - 122), packed[0][index])
            packed[1][index] = jnp.where(here, turned(field, 8 * level), packed[1][index])
    odd = odd_tile()
    for index in range(2):
        at = pl.ds(ROWS * index, ROWS)
        to_chip[at, :] = jnp.where(odd, packed[0][index], packed[1][index])
        to_core[at, :] = jnp.where(odd, packed[1][index], packed[0][index])
    to_core[64:72, :] = folded(swung(below, odd, 0, -122))


def send_heating(got, trigger, closure, weights, from_core, raw, out, to_chip, stacked):
    me = lax.axis_index("lev")
    flags = trigger[pl.ds(BAND * me, BAND), :].astype(F32)
    scheme = closure[pl.ds(BAND * me, BAND), :]
    for row in range(BAND):
        chosen = [
            jnp.broadcast_to(
                jnp.where(scheme[row : row + 1] == s, flags[row : row + 1], 0.0), (OWN, LANES)
            ).astype(BF16)
            for s in range(3)
        ]
        columns = pl.ds(LANES * row, LANES)
        for peer in range(PEERS):
            block = got[peer, pl.ds(OWN * row, OWN), :]
            for s in range(3):
                stacked[pl.ds(LEVELS * s + OWN * peer, OWN), columns] = block * chosen[s]
            stacked[pl.ds(LEVELS * 3 + OWN * peer, OWN), columns] = block
    wide = jnp.concatenate([weights[s] for s in range(4)], axis=1)
    answer = jnp.dot(wide, stacked[...], preferred_element_type=F32).astype(BF16)
    for peer in range(PEERS):
        for row in range(BAND):
            out[peer, pl.ds(OWN * row, OWN), :] = answer[
                OWN * peer : OWN * peer + OWN, LANES * row : LANES * row + LANES
            ]
    core_border = in_low_half(from_core[64:72, :])
    higher = jnp.zeros((8, LANES), F32)
    beyond = jnp.zeros((8, LANES), F32)
    for peer in reversed(range(PEERS)):
        send_parts(out, peer, jnp.where(top_half(), higher, core_border))
        pair = got[peer, 64:80, :].astype(F32)
        higher = higher + ((pair[0:8] + halves_swapped(pair[0:8])) + pair[8:16])
        part = halves_swapped(pair[8:16]) + pltpu.roll(pair[8:16], 2, 0)
        beyond = beyond + jnp.where(me < peer, 1.0, 0.0) * part
    border = unfolded(from_two_rows(beyond))
    border = jnp.where(lanes_of(border.shape) < 6, border, 0.0)
    for shift in (8, 16, 32, 64):
        border = border + turned(border, shift)
    to_chip[0:32, :] = raw[0:32, :] + border
    to_chip[32:64, :] = raw[32:64, :]


def slot(level):
    return 32 * (level % 4)


def halo_lanes(right):
    lane = lanes_of((ROWS, LANES)) & 31
    start = by_side(right, 12, 0)
    return (lane >= start) & (lane < start + 6)


def in_slot(level):
    lane = lanes_of((ROWS, LANES))
    return (lane >= slot(level)) & (lane < slot(level) + 32)


def band(level):
    return pl.ds(ROWS * (level // 4), ROWS)


def put_halos(base, halos, right, edge, extra):
    is_halo = halo_lanes(right)
    for first in range(0, OWN, 4):
        value = base[band(first), :]
        for level in range(first, first + 4):
            here = slot(level)
            halo = swung(halos, right, here + 12 - 8 * level, here - 8 * level)
            value = jnp.where(is_halo & in_slot(level), halo, value)
        edge[band(first), :] = value if extra is None else value + extra


def evolve(p, w):
    p[...], w[...] = substeps(p[...], w[...])


def edge_lanes(right):
    lane = lanes_of((ROWS, LANES))
    start = by_side(right, 122, 0)
    return (lane >= start) & (lane < start + 6)


def edge_of(edge, level, right):
    return swung(edge[band(level), :], right, 116 - slot(level), -6 - slot(level))


def in_every_slot(field, right, if_right, if_left, kept):
    out = None
    for level in range(4):
        moved = swung(field, right, slot(level) + if_right, slot(level) + if_left)
        out = moved if out is None else jnp.where(in_slot(level), moved, out)
    return jnp.where(kept, out, 0.0)


def local_substeps(theta, thickness, wind, surface, out_p, out_w, chip_p, chip_w, core_p, core_w):
    chip_right = odd_tile()
    core_right = jnp.logical_not(chip_right)
    ground = surface[...]
    below = jnp.zeros((ROWS, LANES), F32)
    packed = None
    for level in reversed(range(OWN)):
        at = pl.ds(level * ROWS, ROWS)
        thermal = theta[at, :] * thickness[at, :] * SCALE
        fields = (ground + (below + 0.5 * thermal), wind[at, :])
        below = below + thermal
        out_p[at, :] = fields[0]
        here = slot(level)
        if level % 4 == 3:
            packed = [jnp.zeros((ROWS, LANES), F32)] * 4
        for i in range(2):
            for j, right in ((0, chip_right), (2, core_right)):
                side = swung(fields[i], right, here - 116, here + 6)
                packed[i + j] = jnp.where(in_slot(level), side, packed[i + j])
        if level % 4 == 0:
            for ref, value in zip((chip_p, chip_w, core_p, core_w), packed):
                ref[band(level), :] = value
    out_p[...], out_w[...] = substeps(out_p[...], wind[...])


def middle(
    got, from_core, local_p, local_w, chip_p, core_p, core_w, out_h, out_p, out_w, out_chip, edge_p, edge_w, rows_first
):
    me = lax.axis_index("lev")
    chip_right = odd_tile()
    core_right = jnp.logical_not(chip_right)
    beyond = jnp.zeros((8, LANES), F32)
    pieces = []
    for peer in range(PEERS):
        piece = got_parts(got, peer)
        pieces.append(piece)
        beyond = beyond + jnp.where(me < peer, 1.0, 0.0) * piece
    higher = jnp.concatenate(
        [
            jnp.where(top_half(), pieces[2 * group], halves_swapped(pieces[2 * group + 1]))
            for group in range(4)
        ]
    )
    border = unfolded(from_low_half(beyond))
    is_halo = halo_lanes(core_right)
    extra = in_every_slot(higher, core_right, -116, 6, jnp.logical_not(is_halo))
    extra = extra + in_every_slot(border, core_right, 12, 0, is_halo)
    put_halos(core_p, from_core[0:32, :], core_right, edge_p, extra)
    put_halos(core_w, from_core[32:64, :], core_right, edge_w, None)
    edge_p[128:160, :] = higher
    edge_w[128:160, :] = jnp.zeros((ROWS, LANES), F32)
    evolve(edge_p, edge_w)
    add_p = edge_p[128:160, :]
    add_w = edge_w[128:160, :]
    fixed = edge_lanes(core_right)
    for level in range(OWN):
        at = pl.ds(level * ROWS, ROWS)
        out_p[at, :] = jnp.where(fixed, edge_of(edge_p, level, core_right), local_p[at, :] + add_p)
        out_w[at, :] = jnp.where(fixed, edge_of(edge_w, level, core_right), local_w[at, :] + add_w)
    extra = in_every_slot(higher, chip_right, -116, 6, jnp.logical_not(halo_lanes(chip_right)))
    for first in range(0, OWN, 4):
        out_chip[band(first), :] = chip_p[band(first), :] + extra
    for peer in range(PEERS):
        rows_first[pl.ds(64 * peer, 64), :] = got[peer, 0:64, :].astype(F32)
    for level in range(OWN):
        out_h[pl.ds(level * ROWS, ROWS), :] = rows_first[pl.ds(level, ROWS, stride=OWN), :].astype(
            BF16
        )


def finish(
    from_chip, heating, local_p, local_w, chip_p, chip_w, out_p, out_w, out_h, edge_p, edge_w, done_p, done_w, sems
):
    copies = [pltpu.make_async_copy(heating, out_h, sems.at[8])]
    copies[0].start()
    right = odd_tile()
    put_halos(chip_p, from_chip[0:32, :], right, edge_p, None)
    put_halos(chip_w, from_chip[32:64, :], right, edge_w, None)
    evolve(edge_p, edge_w)
    fixed = edge_lanes(right)
    for index, (edge, local, done, out) in enumerate(
        ((edge_p, local_p, done_p, out_p), (edge_w, local_w, done_w, out_w))
    ):
        for level in range(OWN):
            at = pl.ds(level * ROWS, ROWS)
            done[at, :] = jnp.where(fixed, edge_of(edge, level, right), local[at, :])
        copy = pltpu.make_async_copy(done, out, sems.at[index])
        copy.start()
        copies.append(copy)
    for copy in copies:
        copy.wait()


def call(kernel, outs, scratch=(), flops=100000, moved=1000000, room=8 << 20, own_copies=False):
    held = [pltpu.VMEM(s, d) for s, d in scratch]
    more = {}
    if own_copies:
        held.append(pltpu.SemaphoreType.DMA((9,)))
        more = dict(out_specs=tuple(pl.BlockSpec(memory_space=pl.ANY) for _ in outs))
    return pl.pallas_call(
        kernel,
        out_shape=tuple(jax.ShapeDtypeStruct(s, d) for s, d in outs),
        scratch_shapes=held,
        compiler_params=pltpu.CompilerParams(vmem_limit_bytes=room),
        cost_estimate=pl.CostEstimate(flops=flops, bytes_accessed=moved, transcendentals=0),
        **more,
    )


def coupled(theta, thickness, wind, surface, trigger, closure, closure_weights):
    flat = (OWN * ROWS, LANES)
    theta, thickness, wind = (x.reshape(flat) for x in (theta, thickness, wind))
    tiles = lax.axis_size("tile")
    (columns,) = call(send_columns, [((PEERS, 80, LANES), BF16)], room=60 << 20)(
        theta, thickness
    )
    columns = lax.all_to_all(columns, "lev", 0, 0, tiled=True)
    raw, to_core = call(send_borders, [((64, LANES), F32), ((72, LANES), F32)])(
        theta, thickness, wind, surface
    )
    between = [((t + 1) % tiles, (t + 2) % tiles) for t in range(0, tiles, 2)]
    within = [(t, t + 1) for t in range(0, tiles, 2)]
    packed = (4 * ROWS, LANES)
    from_core = lax.ppermute(to_core, "tile", within + [(b, a) for a, b in within])
    local_p, local_w, chip_p, chip_w, core_p, core_w = call(
        local_substeps, [(flat, F32)] * 2 + [(packed, F32)] * 4, flops=20000000
    )(theta, thickness, wind, surface)
    heats, to_chip = call(
        send_heating,
        [((PEERS, PIECE, LANES), BF16), ((64, LANES), F32)],
        [((512, 512), BF16)],
        flops=70000000,
    )(columns, trigger, closure, closure_weights, from_core, raw)
    heats = lax.all_to_all(heats, "lev", 0, 0, tiled=True)
    from_chip = lax.ppermute(to_chip, "tile", between + [(b, a) for a, b in between])
    heating, local_p, local_w, chip_p = call(
        middle,
        [(flat, BF16), (flat, F32), (flat, F32), (packed, F32)],
        [((5 * ROWS, LANES), F32)] * 2 + [(flat, F32)],
    )(heats, from_core, local_p, local_w, chip_p, core_p, core_w)
    pressure, wind_next, heating = call(
        finish,
        [(flat, F32), (flat, F32), (flat, BF16)],
        [(packed, F32)] * 2 + [(flat, F32)] * 2,
        own_copies=True,
    )(from_chip, heating, local_p, local_w, chip_p, chip_w)
    shape = (OWN, ROWS, LANES)
    return pressure.reshape(shape), wind_next.reshape(shape), heating.reshape(shape)


def solution(mesh):
    in_specs = (
        P("lev", None, "tile"),
        P("lev", None, "tile"),
        P("lev", None, "tile"),
        P(None, "tile"),
        P(None, "tile"),
        P(None, "tile"),
        P(),
    )
    out_specs = (P("lev", None, "tile"), P("lev", None, "tile"), P("lev", None, "tile"))
    return jax.shard_map(
        coupled, mesh=mesh, in_specs=in_specs, out_specs=out_specs, check_vma=False
    )
```
